32 devices in a mesh: clip: 4 (over y, x), seq: 8 (over z, core).
Axes of the slice: x: 2, y: 2, z: 4, core: 2. Of those that a mesh axis runs over, the one named last changes fastest.
Arguments:
- inputs: bfloat16 [16, 8, 196, 768], P('clip', 'seq'), may hold values from -6 to 6
- norm_gains: bfloat16 [3, 768], P(None, ('clip', 'seq')), may hold values from 0.25 to 1.75
- norm_biases: bfloat16 [3, 768], P(None, ('clip', 'seq')), may hold values from -2 to 2
- qkv_weights: bfloat16 [2, 768, 2304], P(None, ('clip', 'seq')), may hold values from -0.21875 to 0.21875
- qv_biases: bfloat16 [2, 2, 768], P(None, None, ('clip', 'seq')), may hold values from -2 to 2
- out_weights: bfloat16 [2, 768, 768], P(None, ('clip', 'seq')), may hold values from -0.875 to 0.875
- out_biases: bfloat16 [2, 768], P(None, ('clip', 'seq')), may hold values from -2 to 2
- up_weight: bfloat16 [768, 3072], P(('clip', 'seq')), may hold values from -0.21875 to 0.21875
- up_bias: bfloat16 [3072], P(('clip', 'seq')), may hold values from -2 to 2
- down_weight: bfloat16 [3072, 768], P(('clip', 'seq')), may hold values from -0.109375 to 0.109375
- down_bias: bfloat16 [768], P(('clip', 'seq')), may hold values from -2 to 2
- out_grad: bfloat16 [16, 8, 196, 768], P('clip', 'seq'), may hold values from -6 to 6
Outputs:
- layer_out: bfloat16 [16, 8, 196, 768], P('clip', 'seq')
- input_grad: float32 [16, 8, 196, 768], P('clip', 'seq')
- norm_gains_grad: float32 [3, 768], P(None, ('clip', 'seq'))
- norm_biases_grad: float32 [3, 768], P(None, ('clip', 'seq'))
- qkv_weights_grad: float32 [2, 768, 2304], P(None, ('clip', 'seq'))
- qv_biases_grad: float32 [2, 2, 768], P(None, None, ('clip', 'seq'))
- out_weights_grad: float32 [2, 768, 768], P(None, ('clip', 'seq'))
- out_biases_grad: float32 [2, 768], P(None, ('clip', 'seq'))
- up_weight_grad: float32 [768, 3072], P(('clip', 'seq'))
- up_bias_grad: float32 [3072], P(('clip', 'seq'))
- down_weight_grad: float32 [3072, 768], P(('clip', 'seq'))
- down_bias_grad: float32 [768], P(('clip', 'seq'))
The draws below stay inside these ranges and needn't reach their ends.
All inputs are finite; a program needn't handle non-finite values.
Results may differ from the reference program's by a relative error of at most 0.022.
Values may be sent and summed in bfloat16 or wider, within the bound.
No kernel may reach another device: no remote copies, remote signals or barrier semaphores. Data moves between devices by JAX's collectives and lax.ppermute only.
A program may use at most 256 MiB of HBM per device.

```python
import jax
import jax.numpy as jnp
from jax import lax

D = 768
HEADS = 12
HEAD_DIM = 64
FF = 3072
PLACES = 196
FRAMES = 8
CLIPS = 16
CAP = 25
N_SEQ = 8


def block_scale(key, dims, split, least, top_value):
    level, own = 1.0, jax.random.fold_in(key, 6)
    for position, blocks in split:
        heights = jnp.exp(jax.random.uniform(jax.random.fold_in(own, position), (blocks,), jnp.float32, least / len(split), top_value / len(split)))
        level = level * jnp.repeat(heights, dims[position] // blocks).reshape([-1 if axis == position else 1 for axis in range(len(dims))])
    return level


def gaussian(rng, extent, deviation, most, shards=(), kind=jnp.bfloat16):
    drawn = deviation * jax.random.normal(rng, extent, jnp.float32)
    if shards:
        drawn = drawn * block_scale(rng, extent, shards, -0.22, 0.18)
    return jnp.clip(drawn, -most, most).astype(kind)


def setup_inputs(seed: int = 0) -> dict:
    seeds = jax.random.split(jax.random.key(seed), 13)
    inputs = gaussian(seeds[0], (CLIPS, FRAMES, PLACES, D), 1.0, 6.0, ((0, 4), (1, 8)))
    norm_gains = jnp.clip(1.0 + 0.15 * jax.random.normal(seeds[1], (3, D), jnp.float32), 0.25, 1.75).astype(jnp.bfloat16)
    norm_biases = gaussian(seeds[2], (3, D), 0.3, 2.0, ((1, 32),))
    qkv_weights = gaussian(seeds[3], (2, D, 3 * D), D ** -0.5, 0.21875, ((1, 32),))
    qv_biases = gaussian(seeds[4], (2, 2, D), 0.3, 2.0, ((2, 32),))
    out_weights = gaussian(seeds[5], (2, D, D), (D // 16) ** -0.5, 0.875, ((1, 32),))
    out_biases = gaussian(seeds[6], (2, D), 0.3, 2.0, ((1, 32),))
    up_weight = gaussian(seeds[7], (D, FF), D ** -0.5, 0.21875, ((0, 32),))
    up_bias = gaussian(seeds[8], (FF,), 0.3, 2.0, ((0, 32),))
    down_weight = gaussian(seeds[9], (FF, D), FF ** -0.5, 0.109375, ((0, 32),))
    down_bias = gaussian(seeds[10], (D,), 0.3, 2.0, ((0, 32),))
    out_grad = gaussian(seeds[11], (CLIPS, FRAMES, PLACES, D), 1.0, 6.0, ((0, 4), (1, 8)))
    return dict(inputs=inputs, norm_gains=norm_gains, norm_biases=norm_biases, qkv_weights=qkv_weights, qv_biases=qv_biases, out_weights=out_weights, out_biases=out_biases, up_weight=up_weight, up_bias=up_bias, down_weight=down_weight, down_bias=down_bias, out_grad=out_grad)


@jax.custom_vjp
def low(v):
    return lax.optimization_barrier(v.astype(jnp.bfloat16)).astype(jnp.float32)

@jax.custom_vjp
def low_back(v):
    return v

def low_keep(v):
    return (low(v), None)

def low_pass(kept, grad):
    return (grad,)

def back_keep(v):
    return (v, None)

def back_low(kept, grad):
    return (low(grad),)
low.defvjp(low_keep, low_pass)
low_back.defvjp(back_keep, back_low)
EPSILON = 1e-05
HIGHEST = lax.Precision.HIGHEST

def both_low(values):
    return low(low_back(values))

def normalize(values, gain, shift):
    center = values - lax.optimization_barrier(jnp.mean(values, axis=-1, keepdims=True))
    spread = lax.optimization_barrier(jnp.mean(center * center, axis=-1, keepdims=True))
    return center * lax.rsqrt(spread + EPSILON) * gain + shift

def split_heads(values):
    return values.reshape(values.shape[0], values.shape[1], HEADS, HEAD_DIM)

def attend(normed, qkv_weight, qv_bias, out_weight, out_bias):
    width = normed.shape[-1]
    joined = jnp.einsum('bsd,de->bse', normed, qkv_weight, precision=HIGHEST)
    query = both_low(joined[..., :width] + qv_bias[0])
    key = both_low(joined[..., width:2 * width])
    value = both_low(joined[..., 2 * width:] + qv_bias[1])
    scores = jnp.einsum('bqhe,bkhe->bhqk', split_heads(query), split_heads(key), precision=HIGHEST) * HEAD_DIM ** (-0.5)
    scores = low_back(scores)
    attn_probs = low(jax.nn.softmax(scores, axis=-1))
    mixed = jnp.einsum('bhqk,bkhe->bqhe', attn_probs, split_heads(value), precision=HIGHEST)
    mixed = both_low(mixed.reshape(normed.shape))
    projected = jnp.einsum('bsd,de->bse', mixed, out_weight, precision=HIGHEST) + out_bias
    return low_back(projected)

def place_groups(places, groups, capacity):
    larger = places - groups * (capacity - 1)
    boundary = larger * capacity
    narrow = max(capacity - 1, 1)
    place_ids = jnp.arange(places, dtype=jnp.int32)
    return jnp.where(place_ids < boundary, place_ids // capacity, larger + (place_ids - boundary) // narrow).astype(jnp.int32)

def slot_tables(owner):
    group_ids = jnp.arange(N_SEQ, dtype=jnp.int32)
    member = owner[None, :] == group_ids[:, None]
    counts = lax.optimization_barrier(jnp.sum(member.astype(jnp.int32), axis=1))
    starts = lax.optimization_barrier(jnp.sum((owner[None, :] < group_ids[:, None]).astype(jnp.int32), axis=1))
    column = jnp.arange(CAP, dtype=jnp.int32)
    slot_valid = column[None, :] < counts[:, None]
    slot_place = jnp.minimum(starts[:, None] + column[None, :], PLACES - 1).astype(jnp.int32)
    own_start = lax.optimization_barrier(jnp.sum(jnp.where(member, starts[:, None], 0), axis=0)).astype(jnp.int32)
    back_index = (owner * CAP + jnp.arange(PLACES, dtype=jnp.int32) - own_start).astype(jnp.int32)
    return (slot_place, slot_valid, back_index)

def layer(clip_in, params, slot_place, slot_valid, back_index):
    gains, shifts, qkv_all, qv_all, outw_all, outb_all, up_matrix, up_shift, down_matrix, down_shift = params
    frames, places, width = clip_in.shape
    groups, capacity = slot_valid.shape
    normed_one = low(normalize(clip_in, gains[0], shifts[0]))
    middle = both_low(clip_in + attend(normed_one, qkv_all[0], qv_all[0], outw_all[0], outb_all[0]))
    picked = jnp.take(middle, slot_place.reshape(-1), axis=1).reshape(frames, groups, capacity, width)
    picked = jnp.transpose(picked, (1, 2, 0, 3)) * slot_valid[:, :, None, None].astype(clip_in.dtype)
    temporal_in = picked.reshape(groups * capacity, frames, width)
    normed_two = low(normalize(temporal_in, gains[1], shifts[1]))
    later = both_low(temporal_in + attend(normed_two, qkv_all[1], qv_all[1], outw_all[1], outb_all[1]))
    later = jnp.transpose(later.reshape(groups, capacity, frames, width), (2, 0, 1, 3)).reshape(frames, groups * capacity, width)
    mlp_in = jnp.take(later, back_index, axis=1)
    normed_three = low(normalize(mlp_in, gains[2], shifts[2]))
    hidden = low_back(jnp.einsum('bsd,df->bsf', normed_three, up_matrix, precision=HIGHEST) + up_shift)
    active = low(jax.nn.gelu(hidden, approximate=False))
    branch = low_back(jnp.einsum('bsf,fd->bsd', active, down_matrix, precision=HIGHEST) + down_shift)
    return mlp_in + branch

def reference(inputs, norm_gains, norm_biases, qkv_weights, qv_biases, out_weights, out_biases, up_weight, up_bias, down_weight, down_bias, out_grad):
    params = tuple((array.astype(jnp.float32) for array in (norm_gains, norm_biases, qkv_weights, qv_biases, out_weights, out_biases, up_weight, up_bias, down_weight, down_bias)))
    slot_place, slot_valid, back_index = slot_tables(place_groups(PLACES, N_SEQ, CAP))

    def forward(clip_rows, weights):
        return layer(clip_rows, weights, slot_place, slot_valid, back_index)

    def one_clip(running, pair_in):
        clip_in, clip_grad = pair_in
        result, pull_back = jax.vjp(forward, clip_in.astype(jnp.float32), params)
        clip_input_grad, weight_grads = pull_back(clip_grad.astype(jnp.float32))
        running = tuple((before + update for before, update in zip(running, weight_grads)))
        return (running, (result.astype(jnp.bfloat16), clip_input_grad))
    zeros_start = tuple((jnp.zeros_like(array) for array in params))
    totals, (outputs, input_grads) = lax.scan(one_clip, zeros_start, (inputs, out_grad))
    return (outputs, input_grads, totals[0], totals[1], totals[2], totals[3], totals[4], totals[5], totals[6], totals[7], totals[8], totals[9])
```

```python
import functools

import jax
import jax.numpy as jnp
from jax import lax
from jax.experimental import pallas as pl
from jax.experimental.pallas import tpu as pltpu
from jax.sharding import PartitionSpec as P

HEAD_DIM = 64
EPSILON = 1e-05
AXES = ("clip", "seq")
LANES = 128


def to_low(values):
    return values.astype(jnp.bfloat16)


class Layout:
    def __init__(self):
        self.seq = lax.axis_size("seq")
        self.clip = lax.axis_size("clip")
        self.count = self.seq * self.clip
        seq_bits = self.seq.bit_length() - 1
        clip_bits = self.clip.bit_length() - 1
        self.core = [0]
        self.z = list(range(1, seq_bits))
        self.clip_a = list(range(seq_bits, seq_bits + clip_bits))
        half = clip_bits // 2
        self.clip_b = self.clip_a[half:] + self.clip_a[:half]
        self.me = lax.axis_index("clip") * self.seq + lax.axis_index("seq")

    def swap(self, array, bit):
        pairs = [(d, d ^ (1 << bit)) for d in range(self.count)]
        return lax.ppermute(array, AXES, pairs)

    def own_bit(self, bit):
        return lax.rem(self.me // (1 << bit), 2)


def order_of(layout, half):
    clip = layout.clip_a if half == 0 else layout.clip_b
    return layout.z + clip + layout.core


def position(relative_bits, bits):
    return sum(value * (1 << place) for place, value in enumerate(relative_bits[b] for b in bits))


def gather_blocks(layout, shard):
    rows, columns = shard.shape
    cut = columns // (2 * LANES) * LANES
    held = shard[None]
    for bit in layout.z:
        held = jnp.concatenate([held, layout.swap(held, bit)])
    halves = []
    for half, part in enumerate((held[:, :, :cut], held[:, :, cut:])):
        for bit in order_of(layout, half)[len(layout.z) :]:
            part = jnp.concatenate([part, layout.swap(part, bit)])
        halves.append(part)
    return halves


def place_table(layout, half):
    bits = order_of(layout, half)
    own = [layout.own_bit(b) for b in range(len(bits))]
    table = []
    for k in range(layout.count):
        relative = [own[b] if (k >> b) % 2 == 0 else 1 - own[b] for b in range(len(bits))]
        table.append(position(relative, bits))
    return jnp.stack(table).astype(jnp.int32)


def assemble_kernel(count, cut, table_ref, left_ref, right_ref, out_ref, sem):
    copies = []
    for k in range(count):
        copies.append(
            pltpu.make_async_copy(
                left_ref.at[table_ref[0, k]], out_ref.at[k, :, pl.ds(0, cut)], sem.at[2 * k]
            )
        )
        copies.append(
            pltpu.make_async_copy(
                right_ref.at[table_ref[1, k]],
                out_ref.at[k, :, pl.ds(cut, out_ref.shape[2] - cut)],
                sem.at[2 * k + 1],
            )
        )
    for copy in copies:
        copy.start()
    for copy in copies:
        copy.wait()


def assemble(layout, halves, tables):
    left, right = halves
    count, rows, cut = left.shape
    columns = cut + right.shape[2]
    if rows % 8:
        left, right = (jnp.take(h, tables[i], axis=0) for i, h in enumerate(halves))
        return jnp.concatenate([left, right], axis=2).reshape(count * rows, columns)
    whole = pl.pallas_call(
        functools.partial(assemble_kernel, count, cut),
        out_shape=jax.ShapeDtypeStruct((count, rows, columns), left.dtype),
        in_specs=[
            pl.BlockSpec(memory_space=pltpu.SMEM),
            pl.BlockSpec(memory_space=pl.ANY),
            pl.BlockSpec(memory_space=pl.ANY),
        ],
        out_specs=pl.BlockSpec(memory_space=pltpu.VMEM),
        scratch_shapes=[pltpu.SemaphoreType.DMA((2 * count,))],
        cost_estimate=pl.CostEstimate(
            flops=0, transcendentals=0, bytes_accessed=2 * count * rows * columns * 2
        ),
        name="assemble",
    )(tables, left, right)
    return whole.reshape(count * rows, columns)


def split_kernel(count, cut, table_ref, whole_ref, left_ref, right_ref, sem):
    copies = []
    for k in range(count):
        copies.append(
            pltpu.make_async_copy(
                whole_ref.at[k, :, pl.ds(0, cut)], left_ref.at[table_ref[0, k]], sem.at[2 * k]
            )
        )
        copies.append(
            pltpu.make_async_copy(
                whole_ref.at[k, :, pl.ds(cut, whole_ref.shape[2] - cut)],
                right_ref.at[table_ref[1, k]],
                sem.at[2 * k + 1],
            )
        )
    for copy in copies:
        copy.start()
    for copy in copies:
        copy.wait()


def split_blocks(layout, whole, tables):
    count = layout.count
    rows, columns = whole.shape[0] // count, whole.shape[1]
    cut = columns // (2 * LANES) * LANES
    blocks = whole.reshape(count, rows, columns)
    if rows % 8:
        parts = []
        for half, part in enumerate((blocks[:, :, :cut], blocks[:, :, cut:])):
            parts.append(jnp.zeros_like(part).at[tables[half]].set(part))
        return parts
    return pl.pallas_call(
        functools.partial(split_kernel, count, cut),
        out_shape=(
            jax.ShapeDtypeStruct((count, rows, cut), whole.dtype),
            jax.ShapeDtypeStruct((count, rows, columns - cut), whole.dtype),
        ),
        in_specs=[
            pl.BlockSpec(memory_space=pltpu.SMEM),
            pl.BlockSpec(memory_space=pltpu.VMEM),
        ],
        out_specs=[pl.BlockSpec(memory_space=pl.ANY)] * 2,
        scratch_shapes=[pltpu.SemaphoreType.DMA((2 * count,))],
        cost_estimate=pl.CostEstimate(
            flops=0, transcendentals=0, bytes_accessed=2 * count * rows * columns * 2
        ),
        name="split_blocks",
    )(tables, blocks)


def scatter_sum(layout, whole, tables):
    results = []
    for half, part in enumerate(split_blocks(layout, whole, tables)):
        for bit in reversed(order_of(layout, half)):
            middle = part.shape[0] // 2
            arrived = layout.swap(part[middle:], bit)
            part = to_low(part[:middle].astype(jnp.float32) + arrived.astype(jnp.float32))
        results.append(part[0])
    return jnp.concatenate(results, axis=1).astype(jnp.float32)


def exchange(array):
    return lax.all_to_all(array, "seq", split_axis=0, concat_axis=0, tiled=True)


def normalize(values, gain, shift):
    center = values - jnp.mean(values, axis=-1, keepdims=True)
    inverse = lax.rsqrt(jnp.mean(center * center, axis=-1, keepdims=True) + EPSILON)
    unit = center * inverse
    return (unit * gain + shift, unit, inverse)


def normalize_back(upstream, unit, inverse, gain):
    scaled = upstream * gain
    gain_grad = jnp.sum(upstream * unit, axis=(0, 1))
    shift_grad = jnp.sum(upstream, axis=(0, 1))
    inner = (
        scaled
        - jnp.mean(scaled, axis=-1, keepdims=True)
        - unit * jnp.mean(scaled * unit, axis=-1, keepdims=True)
    )
    return (inverse * inner, gain_grad, shift_grad)


def split_heads(values):
    return values.reshape(values.shape[0], values.shape[1], -1, HEAD_DIM)


def score_block(query, key):
    return jnp.einsum(
        "bqhe,bkhe->bhqk", split_heads(query), split_heads(key), preferred_element_type=jnp.float32
    ) * HEAD_DIM ** (-0.5)


def attend_forward(normed_low, weight, qv_bias, out_bias):
    width = normed_low.shape[-1]
    qkv_weight, out_weight = weight[:, : 3 * width], weight[:, 3 * width : 4 * width]
    joined = jnp.einsum("bsd,de->bse", normed_low, qkv_weight, preferred_element_type=jnp.float32)
    query = to_low(joined[..., :width] + qv_bias[0])
    key = to_low(joined[..., width : 2 * width])
    value = to_low(joined[..., 2 * width :] + qv_bias[1])
    scores = score_block(query, key)
    peaked = jnp.max(scores, axis=-1, keepdims=True)
    raised = jnp.exp(scores - peaked)
    summed = jnp.sum(raised, axis=-1, keepdims=True)
    weights_low = to_low(raised / summed)
    mixed = jnp.einsum(
        "bhqk,bkhe->bqhe", weights_low, split_heads(value), preferred_element_type=jnp.float32
    )
    mixed = to_low(mixed.reshape(normed_low.shape))
    projected = (
        jnp.einsum("bsd,de->bse", mixed, out_weight, preferred_element_type=jnp.float32) + out_bias
    )
    return (projected, (query, key, value, mixed, peaked + jnp.log(summed)))


def attend_backward(upstream, normed_low, weight, saved):
    query, key, value, mixed, logsum = saved
    width = normed_low.shape[-1]
    qkv_weight, out_weight = weight[:, : 3 * width], weight[:, 3 * width : 4 * width]
    scale = HEAD_DIM ** (-0.5)
    upstream_low = to_low(upstream)
    out_bias_grad = jnp.sum(upstream_low, axis=(0, 1), dtype=jnp.float32)
    out_weight_grad = jnp.einsum(
        "bsd,bse->de", mixed, upstream_low, preferred_element_type=jnp.float32
    )
    mixed_grad = split_heads(
        to_low(
            jnp.einsum("bse,de->bsd", upstream_low, out_weight, preferred_element_type=jnp.float32)
        )
    )
    probs = jnp.exp(score_block(query, key) - logsum)
    value_grad = jnp.einsum(
        "bhqk,bqhe->bkhe", to_low(probs), mixed_grad, preferred_element_type=jnp.float32
    )
    probs_grad = jnp.einsum(
        "bqhe,bkhe->bhqk", mixed_grad, split_heads(value), preferred_element_type=jnp.float32
    )
    scores_grad = to_low(probs * (probs_grad - jnp.sum(probs * probs_grad, axis=-1, keepdims=True)))
    query_grad = (
        jnp.einsum(
            "bhqk,bkhe->bqhe", scores_grad, split_heads(key), preferred_element_type=jnp.float32
        )
        * scale
    )
    key_grad = (
        jnp.einsum(
            "bhqk,bqhe->bkhe", scores_grad, split_heads(query), preferred_element_type=jnp.float32
        )
        * scale
    )
    flat_shape = normed_low.shape
    joined_grad = to_low(
        jnp.concatenate(
            [
                query_grad.reshape(flat_shape),
                key_grad.reshape(flat_shape),
                value_grad.reshape(flat_shape),
            ],
            axis=-1,
        )
    )
    qv_bias_grad = jnp.stack(
        [
            jnp.sum(joined_grad[..., :width], axis=(0, 1), dtype=jnp.float32),
            jnp.sum(joined_grad[..., 2 * width :], axis=(0, 1), dtype=jnp.float32),
        ]
    )
    qkv_weight_grad = jnp.einsum(
        "bsd,bse->de", normed_low, joined_grad, preferred_element_type=jnp.float32
    )
    normed_grad = jnp.einsum(
        "bse,de->bsd", joined_grad, qkv_weight, preferred_element_type=jnp.float32
    )
    weight_grad = to_low(jnp.concatenate([qkv_weight_grad, out_weight_grad], axis=1))
    return (normed_grad, (weight_grad, qv_bias_grad, out_bias_grad))


def on_device(
    inputs,
    norm_gains,
    norm_biases,
    qkv_weights,
    qv_biases,
    out_weights,
    out_biases,
    up_weight,
    up_bias,
    down_weight,
    down_bias,
    out_grad,
):
    layout = Layout()
    clips, frames_dev, places, width = inputs.shape
    groups = layout.seq
    parts = groups * frames_dev // clips if clips <= groups else 1
    assert frames_dev == 1 and groups % clips == 0 and places % parts == 0
    run = places // parts
    rows = up_weight.shape[0]
    folds = up_weight.shape[1] // width
    tables = jnp.stack([place_table(layout, 0), place_table(layout, 1)])

    columns = [
        norm_gains.T,
        norm_biases.T,
        qv_biases.reshape(-1, rows).T,
        out_biases.T,
        up_bias.reshape(rows, folds),
        down_bias[:, None],
    ]
    small = jnp.concatenate(columns, axis=1)
    small = jnp.pad(small, ((0, 0), (0, LANES - small.shape[1])))
    shard_one = jnp.concatenate([qkv_weights[0], out_weights[0], small], axis=1)
    shard_two = jnp.concatenate([qkv_weights[1], out_weights[1]], axis=1)
    shard_up = jnp.swapaxes(up_weight.reshape(rows, width, folds), 1, 2).reshape(rows, -1)
    shard_down = down_weight.reshape(rows, -1)
    weight_one = assemble(layout, gather_blocks(layout, shard_one), tables)
    weight_two = assemble(layout, gather_blocks(layout, shard_two), tables)
    up_matrix = assemble(layout, gather_blocks(layout, shard_up), tables)
    down_matrix = assemble(layout, gather_blocks(layout, shard_down), tables)
    table = weight_one[:, 4 * width :].T.astype(jnp.float32)
    gains, shifts = table[0:3], table[3:6]
    qv_all = table[6:10].reshape(2, 2, width)
    outb_all = table[10:12]
    up_shift = table[12 : 12 + folds].reshape(-1)
    down_shift = table[12 + folds]

    spatial_in = inputs.astype(jnp.float32).reshape(clips, places, width)
    normed_one, unit_one, inverse_one = normalize(spatial_in, gains[0], shifts[0])
    low_one = to_low(normed_one)
    proj_one, saved_one = attend_forward(low_one, weight_one, qv_all[0], outb_all[0])
    middle_low = to_low(spatial_in + proj_one).reshape(groups, run, width)

    placed = exchange(middle_low)
    temporal_in = jnp.swapaxes(placed, 0, 1).astype(jnp.float32)
    normed_two, unit_two, inverse_two = normalize(temporal_in, gains[1], shifts[1])
    low_two = to_low(normed_two)
    proj_two, saved_two = attend_forward(low_two, weight_two, qv_all[1], outb_all[1])
    mlp_in = to_low(temporal_in + proj_two).astype(jnp.float32)
    normed_three, unit_three, inverse_three = normalize(mlp_in, gains[2], shifts[2])
    low_three = to_low(normed_three)
    hidden = (
        jnp.einsum("bsd,df->bsf", low_three, up_matrix, preferred_element_type=jnp.float32)
        + up_shift
    )
    grown = 0.5 * (1.0 + lax.erf(hidden * 0.5**0.5))
    slope = to_low(grown + hidden * jnp.exp(-0.5 * hidden * hidden) * (2.0 * jnp.pi) ** -0.5)
    active_low = to_low(hidden * grown)
    active_low, slope = lax.optimization_barrier((active_low, slope))
    down_tall = down_matrix.reshape(width, folds, width)
    active_split = active_low.reshape(active_low.shape[:2] + (folds, width))
    branch = (
        jnp.einsum("bsjr,rjn->bsn", active_split, down_tall, preferred_element_type=jnp.float32)
        + down_shift
    )
    last_low = to_low(mlp_in + branch)
    layer_out = exchange(jnp.swapaxes(last_low, 0, 1)).reshape(inputs.shape)

    top_placed = exchange(out_grad.reshape(groups, run, width))
    grad_low = jnp.swapaxes(top_placed, 0, 1)
    top_grad = grad_low.astype(jnp.float32)
    down_bias_grad = jnp.sum(top_grad, axis=(0, 1))
    down_weight_grad = to_low(
        jnp.einsum("bsjr,bsn->rjn", active_split, grad_low, preferred_element_type=jnp.float32)
    ).reshape(width, -1)
    active_grad = jnp.einsum(
        "bsn,rjn->bsjr", grad_low, down_tall, preferred_element_type=jnp.float32
    ).reshape(active_low.shape)
    hidden_grad = to_low(active_grad * slope.astype(jnp.float32))
    up_bias_grad = jnp.sum(hidden_grad, axis=(0, 1), dtype=jnp.float32)
    up_weight_grad = to_low(
        jnp.einsum("bsd,bsf->df", low_three, hidden_grad, preferred_element_type=jnp.float32)
    )
    normed_grad_three = jnp.einsum(
        "bsf,df->bsd", hidden_grad, up_matrix, preferred_element_type=jnp.float32
    )
    back_three, gain_three, shift_three = normalize_back(
        normed_grad_three, unit_three, inverse_three, gains[2]
    )
    temporal_grad = to_low(top_grad + back_three).astype(jnp.float32)
    normed_grad_two, temporal_grads = attend_backward(temporal_grad, low_two, weight_two, saved_two)
    back_two, gain_two, shift_two = normalize_back(normed_grad_two, unit_two, inverse_two, gains[1])
    middle_grad = to_low(temporal_grad + back_two)
    grad_returned = exchange(jnp.swapaxes(middle_grad, 0, 1))
    spatial_grad = grad_returned.reshape(clips, places, width).astype(jnp.float32)
    normed_grad_one, spatial_grads = attend_backward(spatial_grad, low_one, weight_one, saved_one)
    back_one, gain_one, shift_one = normalize_back(normed_grad_one, unit_one, inverse_one, gains[0])
    input_grad = (spatial_grad + back_one).reshape(inputs.shape)

    small_grads = jnp.concatenate(
        [
            jnp.stack([gain_one, gain_two, gain_three, shift_one, shift_two, shift_three]),
            spatial_grads[1],
            temporal_grads[1],
            jnp.stack([spatial_grads[2], temporal_grads[2]]),
            up_bias_grad.reshape(folds, width),
            down_bias_grad[None],
        ]
    )
    small_grads = jnp.pad(small_grads, ((0, LANES - small_grads.shape[0]), (0, 0)))
    down_own = scatter_sum(layout, down_weight_grad, tables)
    up_own = scatter_sum(layout, up_weight_grad, tables)
    two_own = scatter_sum(layout, temporal_grads[0], tables)
    one_own = scatter_sum(
        layout, jnp.concatenate([spatial_grads[0], to_low(small_grads.T)], axis=1), tables
    )
    own = one_own[:, 4 * width :].T
    return (
        layer_out,
        input_grad,
        own[0:3],
        own[3:6],
        jnp.stack([one_own[:, : 3 * width], two_own[:, : 3 * width]]),
        own[6:10].reshape(2, 2, rows),
        jnp.stack([one_own[:, 3 * width : 4 * width], two_own[:, 3 * width :]]),
        own[10:12],
        jnp.swapaxes(up_own.reshape(rows, folds, width), 1, 2).reshape(rows, -1),
        own[12 : 12 + folds].T.reshape(-1),
        down_own.reshape(rows * folds, width),
        own[12 + folds],
    )


def solution(mesh):
    return jax.shard_map(
        on_device,
        mesh=mesh,
        in_specs=(
            P("clip", "seq", None, None),
            P(None, AXES),
            P(None, AXES),
            P(None, AXES, None),
            P(None, None, AXES),
            P(None, AXES, None),
            P(None, AXES),
            P(AXES, None),
            P(AXES),
            P(AXES, None),
            P(AXES),
            P("clip", "seq", None, None),
        ),
        out_specs=(
            P("clip", "seq", None, None),
            P("clip", "seq", None, None),
            P(None, AXES),
            P(None, AXES),
            P(None, AXES, None),
            P(None, None, AXES),
            P(None, AXES, None),
            P(None, AXES),
            P(AXES, None),
            P(AXES),
            P(AXES, None),
            P(AXES),
        ),
        check_vma=False,
    )
```
